512 devices in a mesh: row: 64 (over z, y_lo, x), col: 8 (over y_hi, core).
Axes of the slice: x: 4, y: 8 (y_hi: 4, y_lo: 2; y = y_hi * 2 + y_lo), z: 8, core: 2. Of those that a mesh axis runs over, the one named last changes fastest.
Arguments:
- start_vectors: float32 [262144, 256], P('row', 'col'), may hold values from -6 to 6
- ham_blocks: float32 [2048, 8, 128, 128], P(('row', 'col')), may hold values from -0.1875 to 0.1875
- block_cols: int32 [2048, 8], P(('row', 'col')), may hold values from 0 to 2047, as said below
- block_counts: int32 [2048], P(('row', 'col')), may hold values from 1 to 8, as said below
- check_weights: float32 [256], replicated, may hold values from -0.375 to 0.375
Outputs:
- filtered: float32 [262144, 256], P('row', 'col')
- checksum: float32 [262144], P(('row', 'col'))
The draws below stay inside these ranges and needn't reach their ends.
Inputs may be any that keep to these rules, and one draw needn't show every extreme that they name: `block_cols`: slot j of block row b names block column (b + d) mod 2048 for offsets d that are distinct within the row and lie from -4 to 3; slot 0 names the block row itself (d = 0). Only the first block_counts[b] slots of block row b are part of the operator. The block rows of one thirty-second of the devices (at least one device) hold 8 live slots each, all block rows of such a device alike; every other block row holds 1 to 3.
All inputs are finite; a program needn't handle non-finite values.
Results may differ from the reference program's by a relative error of at most 0.0003.
Values sent between devices are 32-bit elements; how exact they have to be, the bound alone decides.
No kernel may reach another device: no remote copies, remote signals or barrier semaphores. Data moves between devices by JAX's collectives and lax.ppermute only.
A program may use at most 64 MiB of HBM per device.

```python
import jax
import jax.numpy as jnp
from jax import lax

B = 128
K = 256
BRD = 4
REACH = 4
ITERS = 3
CAP = 8
NBR = 2048
N = 262144


def block_pattern(key):
    device_count = NBR // BRD
    heavy_number = max(1, device_count // 32)
    device_order = jax.random.permutation(jax.random.fold_in(key, 101), device_count)
    heavy_devices = jnp.zeros((device_count,), jnp.int32).at[device_order[:heavy_number]].set(1)
    heavy_rows = jnp.repeat(heavy_devices, BRD)
    light_counts = jax.random.randint(jax.random.fold_in(key, 102), (NBR,), 1, 4)
    counts = jnp.where(heavy_rows > 0, CAP, light_counts).astype(jnp.int32)
    random_scores = jax.random.randint(jax.random.fold_in(key, 103), (NBR, CAP), 0, 1 << 20)
    scores = random_scores * CAP + jnp.arange(CAP, dtype=jnp.int32)[None, :]
    scores = scores.at[:, REACH].set(-1)
    chosen = jnp.argsort(scores, axis=1).astype(jnp.int32)
    offsets = chosen - REACH
    columns = jnp.mod(jnp.arange(NBR, dtype=jnp.int32)[:, None] + offsets, NBR).astype(jnp.int32)
    return (columns, counts)


def draw_block_cols(key, part):
    columns, counts = block_pattern(jax.random.fold_in(key, 7))
    return columns


def draw_block_counts(key, part):
    columns, counts = block_pattern(jax.random.fold_in(key, 7))
    return counts


def levels(stream_key, shape, split, smallest, high):
    def one(axis_at, blocks):
        heights = jax.random.uniform(jax.random.fold_in(jax.random.fold_in(stream_key, 6), axis_at), (blocks,), jnp.float32, smallest / len(split), high / len(split))
        return jnp.repeat(jnp.exp(heights), shape[axis_at] // blocks).reshape((-1,) + (1,) * (len(shape) - axis_at - 1))

    level = one(*split[0])
    for cut in split[1:]:
        level = level * one(*cut)
    return level


def scatter_about(stream_key, dims, deviation, reach, cuts=(), held_as=jnp.bfloat16):
    result = deviation * jax.random.normal(stream_key, dims, jnp.float32)
    if cuts:
        result = result * levels(stream_key, dims, cuts, -0.22, 0.18)
    return jnp.clip(result, -reach, reach).astype(held_as)


def setup_inputs(seed: int = 0) -> dict:
    streams_of = jax.random.split(jax.random.key(seed), 6)
    start_vectors = scatter_about(streams_of[0], (N, K), 1.0, 6.0, ((0, 64), (1, 8)), jnp.float32)
    ham_blocks = scatter_about(streams_of[1], (NBR, CAP, B, B), (B * CAP) ** -0.5, 0.1875, ((0, 512),), jnp.float32)
    block_cols = draw_block_cols(jax.random.fold_in(streams_of[5], 71), 0)
    block_counts = draw_block_counts(jax.random.fold_in(streams_of[5], 71), 0)
    check_weights = scatter_about(streams_of[4], (K,), K ** -0.5, 0.375, (), jnp.float32)
    return {"start_vectors": start_vectors, "ham_blocks": ham_blocks, "block_cols": block_cols, "block_counts": block_counts, "check_weights": check_weights}


CENTRE = 0.25
HALF_WIDTH = 1.5


def apply_operator(ham_blocks, block_cols, block_counts, vectors, checks):
    block_size = ham_blocks.shape[2]
    slot_count = ham_blocks.shape[1]
    vector_tiles = vectors.reshape(-1, block_size, vectors.shape[1])
    check_tiles = checks.reshape(-1, block_size)

    def one_row(inputs):
        matrices, columns, live_count = inputs
        live_mask = (jnp.arange(slot_count, dtype=jnp.int32) < live_count).astype(matrices.dtype)
        masked = matrices * live_mask[:, None, None]
        gathered = vector_tiles[columns]
        gathered_check = check_tiles[columns]
        product = jnp.einsum("jab,jbk->ak", masked, gathered, precision=lax.Precision.HIGHEST)
        product_check = jnp.einsum("jab,jb->a", masked, gathered_check, precision=lax.Precision.HIGHEST)
        return product, product_check

    products, product_checks = lax.map(one_row, (ham_blocks, block_cols, block_counts))
    return products.reshape(vectors.shape), product_checks.reshape(checks.shape)


def reference(start_vectors, ham_blocks, block_cols, block_counts, check_weights):
    checks = jnp.dot(start_vectors, check_weights, precision=lax.Precision.HIGHEST, preferred_element_type=jnp.float32)
    previous, previous_check = start_vectors, checks
    image_rows, image_check = apply_operator(ham_blocks, block_cols, block_counts, start_vectors, checks)
    current = (image_rows - CENTRE * start_vectors) / HALF_WIDTH
    current_check = (image_check - CENTRE * checks) / HALF_WIDTH
    for step_index in range(ITERS - 1):
        image_rows, image_check = apply_operator(ham_blocks, block_cols, block_counts, current, current_check)
        following = 2.0 * (image_rows - CENTRE * current) / HALF_WIDTH - previous
        following_check = 2.0 * (image_check - CENTRE * current_check) / HALF_WIDTH - previous_check
        previous, previous_check = current, current_check
        current, current_check = following, following_check
    return current, current_check
```

```python
import functools

import jax
import jax.numpy as jnp
from jax import lax
from jax.experimental import pallas as pl
from jax.experimental.pallas import tpu as pltpu
from jax.sharding import Mesh
from jax.sharding import PartitionSpec as P

REACH = 4
ITERS = 3
CENTRE = 0.25
HALF_WIDTH = 1.5
B = 128
CORES = 2
GROUP = 4
CHECK = 8

VMEM = pl.BlockSpec(memory_space=pltpu.VMEM)
SMEM = pl.BlockSpec(memory_space=pltpu.SMEM)


def split(value):
    high = value.astype(jnp.bfloat16)
    low = (value - high.astype(jnp.float32)).astype(jnp.bfloat16)
    return high, low


def prepare_kernel(total, place, ints_own, ints_other, own, other, rhs, near_list, far_list):
    rows, cap = own.shape[0], own.shape[1]
    core, base = place[0], place[1]
    chip_rows = CORES * rows
    rhs[chip_rows * cap] = jnp.zeros(rhs.shape[1:], rhs.dtype)
    near = jnp.int32(0)
    far = jnp.int32(0)
    for ints, blocks, side in ((ints_own, own, core), (ints_other, other, 1 - core)):
        for row in range(rows):
            chip_row = side * rows + row

            def one(slot, counts, ints=ints, blocks=blocks, row=row, chip_row=chip_row):
                near, far = counts
                high, low = split(blocks[row, slot].T)
                where = chip_row * cap + slot
                rhs[where, :, :B] = high
                rhs[where, :, B:] = low
                column = lax.rem(ints[row, slot] - base + total + total, total)
                is_left = column >= total - REACH
                is_near = column < chip_rows

                @pl.when(is_near)
                def _():
                    near_list[0, near] = chip_row
                    near_list[1, near] = where
                    near_list[2, near] = column

                @pl.when(jnp.logical_not(is_near))
                def _():
                    far_list[0, far] = chip_row
                    far_list[1, far] = where
                    far_list[2, far] = jnp.where(
                        is_left, column - (total - REACH), column - chip_rows + REACH
                    )

                step = is_near.astype(jnp.int32)
                return near + step, far + 1 - step

            near, far = lax.fori_loop(0, ints[row, cap], one, (near, far))
    for entries, used in ((near_list, near), (far_list, far)):
        for extra in range(GROUP - 1):
            entries[0, used + extra] = 0
            entries[1, used + extra] = chip_rows * cap
            entries[2, used + extra] = 0
        entries[3, 0] = lax.div(used + GROUP - 1, GROUP)


def stage(pieces, halves):
    width = halves.shape[1] - 16
    at = 0
    for piece, tiles in pieces:
        for tile in range(tiles):
            high, low = split(piece[tile * width : (tile + 1) * width, :])
            halves[at, :width, :B] = high
            halves[at, :width, B:] = low
            row = piece[tiles * width + tile : tiles * width + tile + 1, :]
            high, low = split(jnp.concatenate([row, jnp.zeros((15, B), jnp.float32)], 0))
            halves[at, width:, :B] = high
            halves[at, width:, B:] = low
            at += 1


def multiply(entries, rhs, halves, total):
    def group(index, carry):
        for member in range(GROUP):
            at = index * GROUP + member
            row = entries[0, at]
            matrix = rhs[entries[1, at]]
            result = jnp.dot(
                halves[entries[2, at]],
                jnp.concatenate([matrix, matrix], 0),
                preferred_element_type=jnp.float32,
            )
            total[row] = total[row] + (result[:, :B] + result[:, B:])
        return carry

    lax.fori_loop(0, entries[3, 0], group, 0)


def near_kernel(tiles, state, entries, rhs, total, halves):
    total[...] = jnp.zeros(total.shape, total.dtype)
    stage([(state, tiles)], halves)
    multiply(entries, rhs, halves, total)


def far_kernel(
    tiles, first, last, state, before, near_total, left, right, entries, rhs, *refs
):
    if last:
        out, out_check, halves, total = refs
    else:
        following, to_left, to_right, halves, total = refs
    width = halves.shape[1] - 16
    right_tiles = REACH - 1
    total[...] = near_total[...]
    stage([(left, REACH), (right, right_tiles)], halves)
    multiply(entries, rhs, halves, total)
    for tile in range(tiles):
        here = slice(tile * width, (tile + 1) * width)
        check = slice(tiles * width + tile, tiles * width + tile + 1)
        pair = []
        for product, at in ((total[tile, :width, :], here), (total[tile, width : width + 1, :], check)):
            value = (product - CENTRE * state[at, :]) * (1.0 / HALF_WIDTH)
            if not first:
                value = 2.0 * value - before[at, :]
            pair.append(value)
        main, row = pair
        if last:
            parts = out.shape[0]
            each = width // parts
            for part in range(parts):
                out[part, tile] = main[part * each : (part + 1) * each, :]
            out_check[tile : tile + 1, :] = row
        else:
            following[here, :] = main
            following[check, :] = row
            if tile < right_tiles:
                to_left[here, :] = main
                spot = right_tiles * width + tile
                to_left[spot : spot + 1, :] = row
            if tile >= tiles - REACH:
                shifted = tile - (tiles - REACH)
                to_right[shifted * width : (shifted + 1) * width, :] = main
                spot = REACH * width + shifted
                to_right[spot : spot + 1, :] = row


def gather_kernel(tiles, arrived, weights, state, to_left, to_right):
    parts, each = arrived.shape[0], arrived.shape[2]
    width = parts * each
    right_tiles = REACH - 1
    for tile in range(tiles):
        row = jnp.zeros((1, B), jnp.float32)
        for part in range(parts):
            value = arrived[part, tile]
            at = part * each
            row = row + jnp.sum(value * weights[at : at + each, :], axis=0, keepdims=True)
            state[tile * width + at : tile * width + at + each, :] = value
            if tile < right_tiles:
                to_left[tile * width + at : tile * width + at + each, :] = value
            if tile >= tiles - REACH:
                shifted = (tile - (tiles - REACH)) * width + at
                to_right[shifted : shifted + each, :] = value
        spot = tiles * width + tile
        state[spot : spot + 1, :] = row
        if tile < right_tiles:
            spot = right_tiles * width + tile
            to_left[spot : spot + 1, :] = row
        if tile >= tiles - REACH:
            spot = REACH * width + tile - (tiles - REACH)
            to_right[spot : spot + 1, :] = row


def call(kernel, shapes, inputs, scratch=(), flops=0, moved=0):
    return pl.pallas_call(
        kernel,
        out_shape=tuple(jax.ShapeDtypeStruct(shape, dtype) for shape, dtype, _ in shapes),
        in_specs=[spec for _, spec in inputs],
        out_specs=tuple(spec for _, _, spec in shapes),
        scratch_shapes=list(scratch),
        compiler_params=pltpu.CompilerParams(vmem_limit_bytes=40 << 20),
        cost_estimate=pl.CostEstimate(flops=flops, bytes_accessed=moved, transcendentals=0),
    )(*[value for value, _ in inputs])


def shift(value, axes, count, steps):
    return lax.ppermute(value, axes, [(at, (at + steps) % count) for at in range(count)])


def per_device(start_vectors, ham_blocks, block_cols, block_counts, check_weights):
    f32 = jnp.float32
    rows, cap = ham_blocks.shape[0], ham_blocks.shape[1]
    parts = lax.axis_size("part")
    chips = lax.axis_size(("row", "part"))
    core = lax.axis_index("core")
    chip = lax.axis_index(("row", "part"))
    tiles = CORES * rows
    total = chips * tiles
    each = start_vectors.shape[1]
    width = parts * each

    sent = start_vectors.T.reshape(each, parts, tiles, B).transpose(1, 2, 0, 3)
    arrived = lax.all_to_all(sent, "part", split_axis=0, concat_axis=0, tiled=True)
    ints = jnp.concatenate([block_cols, block_counts[:, None]], 1)
    other_ints = shift(ints, "core", CORES, 1)
    other_blocks = shift(ham_blocks, "core", CORES, 1)
    place = jnp.stack([core, chip * tiles]).astype(jnp.int32)
    length = tiles * cap + GROUP

    rhs, near_list, far_list = call(
        functools.partial(prepare_kernel, total),
        (
            ((tiles * cap + 1, B, 2 * B), jnp.bfloat16, VMEM),
            ((4, length), jnp.int32, SMEM),
            ((4, length), jnp.int32, SMEM),
        ),
        [(place, SMEM), (ints, SMEM), (other_ints, SMEM), (ham_blocks, VMEM), (other_blocks, VMEM)],
        flops=10**7,
        moved=8 << 20,
    )
    mine = lax.dynamic_index_in_dim(check_weights.reshape(parts, CORES, each), core, 1, False)
    weights = jnp.broadcast_to(mine.reshape(width, 1), (width, B))
    sizes = [tiles * width + CHECK, (REACH - 1) * width + CHECK, REACH * width + CHECK]
    pieces = tuple(((size, B), f32, VMEM) for size in sizes)
    state, to_left, to_right = call(
        functools.partial(gather_kernel, tiles), pieces, [(arrived, VMEM), (weights, VMEM)]
    )
    before = state
    for step in range(ITERS):
        first, last = step == 0, step == ITERS - 1
        left = shift(to_right, ("row", "part"), chips, 1)
        right = shift(to_left, ("row", "part"), chips, -1)
        (near_total,) = call(
            functools.partial(near_kernel, tiles),
            (((tiles, width + 16, B), f32, VMEM),),
            [(state, VMEM), (near_list, SMEM), (rhs, VMEM)],
            [pltpu.VMEM((tiles, width + 16, 2 * B), jnp.bfloat16)],
            flops=10**9,
            moved=4 << 20,
        )
        shapes = pieces
        if last:
            shapes = (
                ((parts, tiles, each, B), f32, VMEM),
                ((tiles, B), f32, VMEM),
            )
        results = call(
            functools.partial(far_kernel, tiles, first, last),
            shapes,
            [
                (state, VMEM),
                (before, VMEM),
                (near_total, VMEM),
                (left, VMEM),
                (right, VMEM),
                (far_list, SMEM),
                (rhs, VMEM),
            ],
            [
                pltpu.VMEM((2 * REACH - 1, width + 16, 2 * B), jnp.bfloat16),
                pltpu.VMEM((tiles, width + 16, B), f32),
            ],
            flops=10**9,
            moved=4 << 20,
        )
        if last:
            out, out_check = results
        else:
            before = state
            state, to_left, to_right = results
    returned = lax.all_to_all(out, "part", split_axis=0, concat_axis=0, tiled=True)
    checks = out_check + shift(out_check, "core", CORES, 1)
    checks = lax.dynamic_slice_in_dim(checks, core * rows, rows, 0).reshape(rows * B)
    filtered = returned.transpose(2, 0, 1, 3).reshape(each, parts * tiles * B).T
    return filtered, checks


def solution(mesh):
    names = ("row", "part", "core")
    rows, cols = mesh.devices.shape
    finer = Mesh(mesh.devices.reshape(rows, cols // CORES, CORES), names)
    placed = (
        P("row", ("part", "core")),
        P(names, None, None, None),
        P(names, None),
        P(names),
        P(),
    )
    return jax.shard_map(
        per_device,
        mesh=finer,
        in_specs=placed,
        out_specs=(P("row", ("part", "core")), P(names)),
        check_vma=False,
    )
```

```python
import functools

import jax
import jax.numpy as jnp
from jax import lax
from jax.experimental import pallas as pl
from jax.experimental.pallas import tpu as pltpu
from jax.sharding import Mesh
from jax.sharding import PartitionSpec as P

REACH = 4
ITERS = 3
CENTRE = 0.25
HALF_WIDTH = 1.5
B = 128
CORES = 2
GROUP = 4
CHECK = 8

VMEM = pl.BlockSpec(memory_space=pltpu.VMEM)
SMEM = pl.BlockSpec(memory_space=pltpu.SMEM)


def split(value):
    high = value.astype(jnp.bfloat16)
    low = (value - high.astype(jnp.float32)).astype(jnp.bfloat16)
    return high, low


def prepare_kernel(total, place, ints_own, ints_other, own, other, rhs, near_list, low_list, high_list):
    rows, cap = own.shape[0], own.shape[1]
    core, base = place[0], place[1]
    chip_rows = CORES * rows
    rhs[chip_rows * cap] = jnp.zeros(rhs.shape[1:], rhs.dtype)
    lists = (near_list, low_list, high_list)
    used = (jnp.int32(0),) * 3
    for ints, blocks, side in ((ints_own, own, core), (ints_other, other, 1 - core)):
        for row in range(rows):
            chip_row = side * rows + row

            def one(slot, used, ints=ints, blocks=blocks, row=row, chip_row=chip_row):
                high, low = split(blocks[row, slot].T)
                where = chip_row * cap + slot
                rhs[where, :, :B] = high
                rhs[where, :, B:] = low
                column = lax.rem(ints[row, slot] - base + total + total, total)
                is_left = column >= total - REACH
                is_right = jnp.logical_and(column >= chip_rows, jnp.logical_not(is_left))
                is_near = column < chip_rows
                targets = (
                    (is_near, chip_row, column),
                    (is_left, chip_row, column - (total - REACH)),
                    (is_right, chip_row - (chip_rows - REACH), column - chip_rows),
                )
                following = []
                for entries, count, (chosen, line, tile) in zip(lists, used, targets):

                    @pl.when(chosen)
                    def _(entries=entries, count=count, line=line, tile=tile):
                        entries[0, count] = line
                        entries[1, count] = where
                        entries[2, count] = tile

                    following.append(count + chosen.astype(jnp.int32))
                return tuple(following)

            used = lax.fori_loop(0, ints[row, cap], one, used)
    for entries, count in zip(lists, used):
        for extra in range(GROUP - 1):
            entries[0, count + extra] = 0
            entries[1, count + extra] = chip_rows * cap
            entries[2, count + extra] = 0
        entries[3, 0] = lax.div(count + GROUP - 1, GROUP)


def stage(pieces, halves):
    width = halves.shape[1] - 16
    at = 0
    for piece in pieces:
        tiles = piece.shape[0] // width
        for tile in range(tiles):
            high, low = split(piece[tile * width : (tile + 1) * width, :])
            halves[at, :width, :B] = high
            halves[at, :width, B:] = low
            row = piece[tiles * width + tile : tiles * width + tile + 1, :]
            high, low = split(jnp.concatenate([row, jnp.zeros((15, B), jnp.float32)], 0))
            halves[at, width:, :B] = high
            halves[at, width:, B:] = low
            at += 1


def multiply(entries, rhs, halves, total):
    def group(index, carry):
        for member in range(GROUP):
            at = index * GROUP + member
            row = entries[0, at]
            matrix = rhs[entries[1, at]]
            result = jnp.dot(
                halves[entries[2, at]],
                jnp.concatenate([matrix, matrix], 0),
                preferred_element_type=jnp.float32,
            )
            total[row] = total[row] + (result[:, :B] + result[:, B:])
        return carry

    lax.fori_loop(0, entries[3, 0], group, 0)


def near_kernel(low, high, entries, rhs, low_total, high_total, halves, total):
    total[...] = jnp.zeros(total.shape, total.dtype)
    stage([low, high], halves)
    multiply(entries, rhs, halves, total)
    low_total[...] = total[:REACH]
    high_total[...] = total[REACH:]


def update(first, tile, state, before, total, width):
    here = slice(tile * width, (tile + 1) * width)
    check = slice(REACH * width + tile, REACH * width + tile + 1)
    pair = []
    for product, at in ((total[tile, :width, :], here), (total[tile, width : width + 1, :], check)):
        value = (product - CENTRE * state[at, :]) * (1.0 / HALF_WIDTH)
        if not first:
            value = 2.0 * value - before[at, :]
        pair.append(value)
    return pair


def far_kernel(first, state, before, near_total, halo, entries, rhs, *refs):
    halves, total = refs[-2:]
    width = halves.shape[1] - 16
    total[...] = near_total[...]
    stage([halo], halves)
    multiply(entries, rhs, halves, total)
    for tile in range(REACH):
        main, row = update(first, tile, state, before, total, width)
        for ref in refs[:-2]:
            tiles = ref.shape[0] // width
            if tile < tiles:
                ref[tile * width : (tile + 1) * width, :] = main
                ref[tiles * width + tile : tiles * width + tile + 1, :] = row


def last_kernel(place, state, before, near_total, halo, entries, rhs, high, *refs):
    halves, total, keep = refs[-3:]
    outs, checks = refs[:-4], refs[-4]
    parts = len(outs)
    width = halves.shape[1] - 16
    each = width // parts
    total[...] = near_total[...]
    stage([halo], halves)
    multiply(entries, rhs, halves, total)
    for tile in range(REACH):
        main, row = update(False, tile, state, before, total, width)
        keep[tile * width : (tile + 1) * width, :] = main
        checks[tile : tile + 1, :] = row
        spot = REACH * width + tile
        checks[REACH + tile : REACH + tile + 1, :] = high[spot : spot + 1, :]
    for steps, out in enumerate(outs):
        at = pl.multiple_of(lax.rem(place[2] + steps, parts) * each, each)
        for tile in range(REACH):
            out[tile] = keep[pl.ds(tile * width + at, each), :]
            out[REACH + tile] = high[pl.ds(tile * width + at, each), :]


def gather_kernel(place, weights, *refs):
    parts = weights.shape[0] // refs[0].shape[1]
    pieces, (low, low_message, high) = refs[:parts], refs[parts:]
    each = pieces[0].shape[1]
    width = parts * each
    for tile in range(2 * REACH):
        row = jnp.zeros((1, B), jnp.float32)
        ref, line = (low, tile) if tile < REACH else (high, tile - REACH)
        spot = REACH * width + line
        for steps, piece in enumerate(pieces):
            at = pl.multiple_of(lax.rem(place[2] - steps + parts, parts) * each, each)
            value = piece[tile]
            row = row + jnp.sum(value * weights[pl.ds(at, each), :], axis=0, keepdims=True)
            ref[pl.ds(line * width + at, each), :] = value
            if tile < REACH - 1:
                low_message[pl.ds(line * width + at, each), :] = value
        ref[spot : spot + 1, :] = row
        if tile < REACH - 1:
            spot = (REACH - 1) * width + tile
            low_message[spot : spot + 1, :] = row


def arrange_kernel(place, vectors, *refs):
    parts, tiles = len(refs), refs[0].shape[0]
    for steps, ref in enumerate(refs):
        at = lax.rem(place[2] + steps, parts) * (tiles * B)
        for tile in range(tiles):
            ref[tile] = vectors[:, pl.ds(pl.multiple_of(at + tile * B, B), B)]


def place_kernel(place, *refs):
    pieces, out = refs[:-1], refs[-1]
    parts, tiles = len(pieces), pieces[0].shape[0]
    for steps, piece in enumerate(pieces):
        at = lax.rem(place[2] - steps + parts, parts) * (tiles * B)
        for tile in range(tiles):
            out[:, pl.ds(pl.multiple_of(at + tile * B, B), B)] = piece[tile]


def call(kernel, shapes, inputs, scratch=(), flops=1, moved=1):
    return pl.pallas_call(
        kernel,
        out_shape=tuple(jax.ShapeDtypeStruct(shape, dtype) for shape, dtype, _ in shapes),
        in_specs=[spec for _, spec in inputs],
        out_specs=tuple(spec for _, _, spec in shapes),
        scratch_shapes=list(scratch),
        compiler_params=pltpu.CompilerParams(vmem_limit_bytes=16 << 20),
        cost_estimate=pl.CostEstimate(flops=flops, bytes_accessed=moved, transcendentals=0),
    )(*[value for value, _ in inputs])


def shift(value, axes, count, steps):
    return lax.ppermute(value, axes, [(at, (at + steps) % count) for at in range(count)])


def per_device(start_vectors, ham_blocks, block_cols, block_counts, check_weights):
    f32 = jnp.float32
    rows, cap = ham_blocks.shape[0], ham_blocks.shape[1]
    parts = lax.axis_size("part")
    chips = lax.axis_size(("row", "part"))
    core = lax.axis_index("core")
    chip = lax.axis_index(("row", "part"))
    tiles = CORES * rows
    total = chips * tiles
    each = start_vectors.shape[1]
    width = parts * each

    place = jnp.stack([core, chip * tiles, lax.axis_index("part")]).astype(jnp.int32)

    def exchange(pieces):
        moved = {steps: shift(pieces[steps], "part", parts, steps) for steps in (2, 1, 3)}
        return [pieces[0]] + [moved[steps] for steps in range(1, parts)]

    piece = ((tiles, each, B), f32, VMEM)
    sent = call(arrange_kernel, (piece,) * parts, [(place, SMEM), (start_vectors.T, VMEM)])
    arrived = exchange(sent)
    ints = jnp.concatenate([block_cols, block_counts[:, None]], 1)
    other_ints = shift(ints, "core", CORES, 1)
    other_blocks = shift(ham_blocks, "core", CORES, 1)
    list_shape = ((4, tiles * cap + GROUP), jnp.int32, SMEM)
    rhs, near_list, low_list, high_list = call(
        functools.partial(prepare_kernel, total),
        (((tiles * cap + 1, B, 2 * B), jnp.bfloat16, VMEM), list_shape, list_shape, list_shape),
        [(place, SMEM), (ints, SMEM), (other_ints, SMEM), (ham_blocks, VMEM), (other_blocks, VMEM)],
    )
    mine = lax.dynamic_index_in_dim(check_weights.reshape(parts, CORES, each), core, 1, False)
    weights = jnp.broadcast_to(mine.reshape(width, 1), (width, B))
    full = ((REACH * width + CHECK, B), f32, VMEM)
    fewer = (((REACH - 1) * width + CHECK, B), f32, VMEM)
    low, low_message, high = call(
        gather_kernel,
        (full, fewer, full),
        [(place, SMEM), (weights, VMEM)] + [(value, VMEM) for value in arrived],
    )
    low_before, high_before = low, high
    part_total = ((REACH, width + 16, B), f32, VMEM)
    for step in range(ITERS):
        first, last = step == 0, step == ITERS - 1
        left = shift(high, ("row", "part"), chips, 1)
        right = shift(low_message, ("row", "part"), chips, -1)
        low_total, high_total = call(
            near_kernel,
            (part_total, part_total),
            [(low, VMEM), (high, VMEM), (near_list, SMEM), (rhs, VMEM)],
            [
                pltpu.VMEM((tiles, width + 16, 2 * B), jnp.bfloat16),
                pltpu.VMEM((tiles, width + 16, B), f32),
            ],
        )

        scratch = [
            pltpu.VMEM((REACH, width + 16, 2 * B), jnp.bfloat16),
            pltpu.VMEM((REACH, width + 16, B), f32),
        ]

        def inputs(state, before, near_total, halo, entries):
            values = (state, before, near_total, halo)
            return [(value, VMEM) for value in values] + [(entries, SMEM), (rhs, VMEM)]

        kernel = functools.partial(far_kernel, first)
        (high_next,) = call(
            kernel, (full,), inputs(high, high_before, high_total, right, high_list), scratch
        )
        low_inputs = inputs(low, low_before, low_total, left, low_list)
        if last:
            *outs, checks = call(
                last_kernel,
                (piece,) * parts + (((tiles, B), f32, VMEM),),
                [(place, SMEM)] + low_inputs + [(high_next, VMEM)],
                scratch + [pltpu.VMEM((REACH * width, B), f32)],
            )
            break
        low_next, low_message = call(kernel, (full, fewer), low_inputs, scratch)
        low_before, high_before = low, high
        low, high = low_next, high_next
    returned = exchange(outs)
    (filtered,) = call(
        place_kernel,
        (((each, parts * tiles * B), f32, VMEM),),
        [(place, SMEM)] + [(value, VMEM) for value in returned],
    )
    checks = checks + shift(checks, "core", CORES, 1)
    checks = lax.dynamic_slice_in_dim(checks, core * rows, rows, 0).reshape(rows * B)
    return filtered.T, checks


def solution(mesh):
    names = ("row", "part", "core")
    rows, cols = mesh.devices.shape
    finer = Mesh(mesh.devices.reshape(rows, cols // CORES, CORES), names)
    placed = (
        P("row", ("part", "core")),
        P(names, None, None, None),
        P(names, None),
        P(names),
        P(),
    )
    return jax.shard_map(
        per_device,
        mesh=finer,
        in_specs=placed,
        out_specs=(P("row", ("part", "core")), P(names)),
        check_vma=False,
    )
```

```python
import functools

import jax
import jax.numpy as jnp
from jax import lax
from jax.experimental import pallas as pl
from jax.experimental.pallas import tpu as pltpu
from jax.sharding import Mesh
from jax.sharding import PartitionSpec as P

REACH = 4
ITERS = 3
CENTRE = 0.25
HALF_WIDTH = 1.5
B = 128
CORES = 2
GROUP = 4
CHECK = 8

VMEM = pl.BlockSpec(memory_space=pltpu.VMEM)
SMEM = pl.BlockSpec(memory_space=pltpu.SMEM)


def split(value):
    high = value.astype(jnp.bfloat16)
    low = (value - high.astype(jnp.float32)).astype(jnp.bfloat16)
    return high, low


def prepare_kernel(total, place, ints_own, ints_other, own, other, rhs, near_list, even_list, odd_list):
    rows, cap = own.shape[0], own.shape[1]
    core, base, swap = place[0], place[1], place[3]
    chip_rows = CORES * rows
    rhs[chip_rows * cap] = jnp.zeros(rhs.shape[1:], rhs.dtype)
    lists = (near_list, even_list, odd_list)
    used = (jnp.int32(0),) * 3
    for ints, blocks, side in ((ints_own, own, core), (ints_other, other, 1 - core)):
        for row in range(rows):
            chip_row = side * rows + row

            def one(slot, used, ints=ints, blocks=blocks, row=row, chip_row=chip_row):
                high, low = split(blocks[row, slot].T)
                where = chip_row * cap + slot
                rhs[where, :, :B] = high
                rhs[where, :, B:] = low
                column = lax.rem(ints[row, slot] - base + total + total, total)
                is_left = column >= total - REACH
                is_near = column < chip_rows
                tile = jnp.where(is_left, column - (total - REACH), column - chip_rows)
                is_even = jnp.logical_and(jnp.logical_not(is_near), is_left == (swap == 0))
                is_odd = jnp.logical_and(jnp.logical_not(is_near), is_left != (swap == 0))
                line = lax.rem(chip_row, REACH)
                targets = (
                    (is_near, lax.rem(chip_row + swap, 2 * REACH), lax.rem(column + swap, 2 * REACH)),
                    (is_even, line, tile),
                    (is_odd, line, tile),
                )
                following = []
                for entries, count, (chosen, line, tile) in zip(lists, used, targets):

                    @pl.when(chosen)
                    def _(entries=entries, count=count, line=line, tile=tile):
                        entries[0, count] = line
                        entries[1, count] = where
                        entries[2, count] = tile

                    following.append(count + chosen.astype(jnp.int32))
                return tuple(following)

            used = lax.fori_loop(0, ints[row, cap], one, used)
    for entries, count in zip(lists, used):
        for extra in range(GROUP - 1):
            entries[0, count + extra] = 0
            entries[1, count + extra] = chip_rows * cap
            entries[2, count + extra] = 0
        entries[3, 0] = lax.div(count + GROUP - 1, GROUP)


def stage(pieces, halves):
    width = halves.shape[1] - 16
    at = 0
    for piece in pieces:
        tiles = piece.shape[0] // width
        for tile in range(tiles):
            high, low = split(piece[tile * width : (tile + 1) * width, :])
            halves[at, :width, :B] = high
            halves[at, :width, B:] = low
            row = piece[tiles * width + tile : tiles * width + tile + 1, :]
            high, low = split(jnp.concatenate([row, jnp.zeros((15, B), jnp.float32)], 0))
            halves[at, width:, :B] = high
            halves[at, width:, B:] = low
            at += 1


def multiply(entries, rhs, halves, total):
    def group(index, carry):
        for member in range(GROUP):
            at = index * GROUP + member
            row = entries[0, at]
            matrix = rhs[entries[1, at]]
            result = jnp.dot(
                halves[entries[2, at]],
                jnp.concatenate([matrix, matrix], 0),
                preferred_element_type=jnp.float32,
            )
            total[row] = total[row] + (result[:, :B] + result[:, B:])
        return carry

    lax.fori_loop(0, entries[3, 0], group, 0)


def near_kernel(even, odd, entries, rhs, even_total, odd_total, halves, total):
    total[...] = jnp.zeros(total.shape, total.dtype)
    stage([even, odd], halves)
    multiply(entries, rhs, halves, total)
    even_total[...] = total[:REACH]
    odd_total[...] = total[REACH:]


def update(first, tile, state, before, total, width):
    here = slice(tile * width, (tile + 1) * width)
    check = slice(REACH * width + tile, REACH * width + tile + 1)
    pair = []
    for product, at in ((total[tile, :width, :], here), (total[tile, width : width + 1, :], check)):
        value = (product - CENTRE * state[at, :]) * (1.0 / HALF_WIDTH)
        if not first:
            value = 2.0 * value - before[at, :]
        pair.append(value)
    return pair


def far_kernel(first, state, before, near_total, halo, entries, rhs, out, halves, total):
    width = halves.shape[1] - 16
    total[...] = near_total[...]
    stage([halo], halves)
    multiply(entries, rhs, halves, total)
    for tile in range(REACH):
        main, row = update(first, tile, state, before, total, width)
        out[tile * width : (tile + 1) * width, :] = main
        out[REACH * width + tile : REACH * width + tile + 1, :] = row


def last_kernel(place, state, before, near_total, halo, entries, rhs, odd, *refs):
    halves, total, keep = refs[-3:]
    outs, checks = refs[:-4], refs[-4]
    parts = len(outs)
    width = halves.shape[1] - 16
    each = width // parts
    total[...] = near_total[...]
    stage([halo], halves)
    multiply(entries, rhs, halves, total)
    even_at, odd_at = place[3], REACH - place[3]
    for tile in range(REACH):
        main, row = update(False, tile, state, before, total, width)
        keep[tile * width : (tile + 1) * width, :] = main
        checks[pl.ds(even_at + tile, 1), :] = row
        spot = REACH * width + tile
        checks[pl.ds(odd_at + tile, 1), :] = odd[spot : spot + 1, :]
    for steps, out in enumerate(outs):
        at = pl.multiple_of(lax.rem(place[2] + steps * place[4] + parts, parts) * each, each)
        for tile in range(REACH):
            out[even_at + tile] = keep[pl.ds(tile * width + at, each), :]
            out[odd_at + tile] = odd[pl.ds(tile * width + at, each), :]


def gather_kernel(place, weights, *refs):
    parts = weights.shape[0] // refs[0].shape[1]
    pieces, halves = refs[:parts], refs[parts:]
    each = pieces[0].shape[1]
    width = parts * each
    for half, start in zip(halves, (place[3], REACH - place[3])):
        for tile in range(REACH):
            row = jnp.zeros((1, B), jnp.float32)
            for steps, piece in enumerate(pieces):
                at = pl.multiple_of(lax.rem(place[2] - steps * place[4] + parts, parts) * each, each)
                value = piece[start + tile]
                row = row + jnp.sum(value * weights[pl.ds(at, each), :], axis=0, keepdims=True)
                half[pl.ds(tile * width + at, each), :] = value
            spot = REACH * width + tile
            half[spot : spot + 1, :] = row


def arrange_kernel(place, vectors, *pieces):
    parts, tiles = len(pieces), pieces[0].shape[0]
    for steps, ref in enumerate(pieces):
        at = lax.rem(place[2] + steps * place[4] + parts, parts) * (tiles * B)
        for tile in range(tiles):
            ref[tile] = vectors[:, pl.ds(pl.multiple_of(at + tile * B, B), B)]


def integers_kernel(cols, counts, ints):
    rows, cap = cols.shape
    lane = lax.broadcasted_iota(jnp.int32, (1, B), 1)
    for row in range(rows):
        value = jnp.where(lane == cap, counts[row], 0)
        for slot in range(cap):
            value = jnp.where(lane == slot, cols[row, slot], value)
        ints[row : row + 1, :] = value


def place_kernel(place, checks, other_checks, *refs):
    pieces, (out, out_check) = refs[:-2], refs[-2:]
    parts, tiles = len(pieces), pieces[0].shape[0]
    for steps, piece in enumerate(pieces):
        at = lax.rem(place[2] - steps * place[4] + parts, parts) * (tiles * B)
        for tile in range(tiles):
            out[:, pl.ds(pl.multiple_of(at + tile * B, B), B)] = piece[tile]
    rows = out_check.shape[0]
    for row in range(rows):
        line = pl.ds(place[0] * rows + row, 1)
        out_check[row : row + 1, :] = checks[line, :] + other_checks[line, :]


def call(kernel, shapes, inputs, scratch=(), flops=1, moved=1):
    return pl.pallas_call(
        kernel,
        out_shape=tuple(jax.ShapeDtypeStruct(shape, dtype) for shape, dtype, _ in shapes),
        in_specs=[spec for _, spec in inputs],
        out_specs=tuple(spec for _, _, spec in shapes),
        scratch_shapes=list(scratch),
        compiler_params=pltpu.CompilerParams(vmem_limit_bytes=16 << 20),
        cost_estimate=pl.CostEstimate(flops=flops, bytes_accessed=moved, transcendentals=0),
    )(*[value for value, _ in inputs])


def shift(value, axes, count, steps):
    return lax.ppermute(value, axes, [(at, (at + steps) % count) for at in range(count)])


def per_device(start_vectors, ham_blocks, block_cols, block_counts, check_weights):
    f32 = jnp.float32
    rows, cap = ham_blocks.shape[0], ham_blocks.shape[1]
    parts = lax.axis_size("part")
    chips = lax.axis_size(("row", "part"))
    core = lax.axis_index("core")
    chip = lax.axis_index(("row", "part"))
    tiles = CORES * rows
    total = chips * tiles
    each = start_vectors.shape[1]
    width = parts * each

    swap = REACH * (1 - core)
    place = jnp.stack([core, chip * tiles, lax.axis_index("part"), swap, 1 - 2 * core]).astype(jnp.int32)

    def pairs(count, steps):
        return [
            (at * CORES + side, (at + steps * (1 - 2 * side)) % count * CORES + side)
            for at in range(count)
            for side in range(CORES)
        ]

    def exchange(pieces):
        moved = [
            lax.ppermute(pieces[steps], ("part", "core"), pairs(parts, steps))
            for steps in range(1, parts)
        ]
        return [pieces[0]] + moved

    def round_chips(value, steps):
        return lax.ppermute(value, ("row", "part", "core"), pairs(chips, steps))

    piece = ((tiles, each, B), f32, VMEM)
    sent = call(arrange_kernel, (piece,) * parts, [(place, SMEM), (start_vectors.T, VMEM)])
    arrived = exchange(sent)
    blocks, columns, counts, _ = lax.optimization_barrier(
        (ham_blocks, block_cols, block_counts, sent[0])
    )
    (ints,) = call(
        integers_kernel, (((rows, B), jnp.int32, VMEM),), [(columns, SMEM), (counts, SMEM)]
    )
    other_ints = shift(ints, "core", CORES, 1)
    other_blocks = shift(blocks, "core", CORES, 1)
    list_shape = ((4, tiles * cap + GROUP), jnp.int32, SMEM)
    rhs, near_list, even_list, odd_list = call(
        functools.partial(prepare_kernel, total),
        (((tiles * cap + 1, B, 2 * B), jnp.bfloat16, VMEM), list_shape, list_shape, list_shape),
        [(place, SMEM), (ints, SMEM), (other_ints, SMEM), (ham_blocks, VMEM), (other_blocks, VMEM)],
    )
    mine = lax.dynamic_index_in_dim(check_weights.reshape(parts, CORES, each), core, 1, False)
    weights = jnp.broadcast_to(mine.reshape(width, 1), (width, B))
    full = ((REACH * width + CHECK, B), f32, VMEM)
    placed, _ = lax.optimization_barrier((place, near_list))
    even, odd = call(
        gather_kernel,
        (full, full),
        [(placed, SMEM), (weights, VMEM)] + [(value, VMEM) for value in arrived],
    )
    even_before, odd_before = even, odd
    part_total = ((REACH, width + 16, B), f32, VMEM)
    scratch = [
        pltpu.VMEM((REACH, width + 16, 2 * B), jnp.bfloat16),
        pltpu.VMEM((REACH, width + 16, B), f32),
    ]
    for step in range(ITERS):
        first, last = step == 0, step == ITERS - 1
        odd_halo = round_chips(even, 1)
        even_halo = round_chips(odd, -1)
        even_total, odd_total = call(
            near_kernel,
            (part_total, part_total),
            [(even, VMEM), (odd, VMEM), (near_list, SMEM), (rhs, VMEM)],
            [
                pltpu.VMEM((tiles, width + 16, 2 * B), jnp.bfloat16),
                pltpu.VMEM((tiles, width + 16, B), f32),
            ],
        )

        def inputs(state, before, near_total, halo, entries):
            values = (state, before, near_total, halo)
            return [(value, VMEM) for value in values] + [(entries, SMEM), (rhs, VMEM)]

        kernel = functools.partial(far_kernel, first)
        (odd_next,) = call(
            kernel, (full,), inputs(odd, odd_before, odd_total, odd_halo, odd_list), scratch
        )
        even_inputs = inputs(even, even_before, even_total, even_halo, even_list)
        if last:
            *outs, checks = call(
                last_kernel,
                (piece,) * parts + (((tiles, B), f32, VMEM),),
                [(place, SMEM)] + even_inputs + [(odd_next, VMEM)],
                scratch + [pltpu.VMEM((REACH * width, B), f32)],
            )
            break
        (even_next,) = call(kernel, (full,), even_inputs, scratch)
        even_before, odd_before = even, odd
        even, odd = even_next, odd_next
    returned = exchange(outs)
    filtered, check_sums = call(
        place_kernel,
        (((each, parts * tiles * B), f32, VMEM), ((rows, B), f32, VMEM)),
        [(place, SMEM), (checks, VMEM), (shift(checks, "core", CORES, 1), VMEM)]
        + [(value, VMEM) for value in returned],
    )
    return filtered.T, check_sums.reshape(rows * B)


def solution(mesh):
    names = ("row", "part", "core")
    rows, cols = mesh.devices.shape
    finer = Mesh(mesh.devices.reshape(rows, cols // CORES, CORES), names)
    placed = (
        P("row", ("part", "core")),
        P(names, None, None, None),
        P(names, None),
        P(names),
        P(),
    )
    return jax.shard_map(
        per_device,
        mesh=finer,
        in_specs=placed,
        out_specs=(P("row", ("part", "core")), P(names)),
        check_vma=False,
    )
```

```python
import functools

import jax
import jax.numpy as jnp
from jax import lax
from jax.experimental import pallas as pl
from jax.experimental.pallas import tpu as pltpu
from jax.sharding import Mesh
from jax.sharding import PartitionSpec as P

REACH = 4
ITERS = 3
CENTRE = 0.25
HALF_WIDTH = 1.5
B = 128
CORES = 2
GROUP = 4
CHECK = 8

VMEM = pl.BlockSpec(memory_space=pltpu.VMEM)
SMEM = pl.BlockSpec(memory_space=pltpu.SMEM)
ANY = pl.BlockSpec(memory_space=pl.ANY)
HBM = pl.BlockSpec(memory_space=pltpu.HBM)


def split(value):
    high = value.astype(jnp.bfloat16)
    low = (value - high.astype(jnp.float32)).astype(jnp.bfloat16)
    return high, low


def prepare_kernel(
    total, place, ints_own, ints_other, source, other, rhs, near_list, even_list, odd_list, own, semaphores
):
    rows, cap = own.shape[0], own.shape[1]
    copies = [
        pltpu.make_async_copy(source.at[row], own.at[row], semaphores.at[row]) for row in range(rows)
    ]
    for copy in copies:
        copy.start()
    core, base, swap = place[0], place[1], place[3]
    chip_rows = CORES * rows
    rhs[chip_rows * cap] = jnp.zeros(rhs.shape[1:], rhs.dtype)
    lists = (near_list, even_list, odd_list)
    used = (jnp.int32(0),) * 3
    for ints, blocks, side in ((ints_other, other, 1 - core), (ints_own, own, core)):
        for row in range(rows):
            if blocks is own:
                copies[row].wait()
            chip_row = side * rows + row

            def one(slot, used, ints=ints, blocks=blocks, row=row, chip_row=chip_row):
                high, low = split(blocks[row, slot].T)
                where = chip_row * cap + slot
                rhs[where, :, :B] = high
                rhs[where, :, B:] = low
                column = lax.rem(ints[row, slot] - base + total + total, total)
                is_left = column >= total - REACH
                is_near = column < chip_rows
                tile = jnp.where(is_left, column - (total - REACH), column - chip_rows)
                is_even = jnp.logical_and(jnp.logical_not(is_near), is_left == (swap == 0))
                is_odd = jnp.logical_and(jnp.logical_not(is_near), is_left != (swap == 0))
                line = lax.rem(chip_row, REACH)
                targets = (
                    (is_near, lax.rem(chip_row + swap, 2 * REACH), lax.rem(column + swap, 2 * REACH)),
                    (is_even, line, tile),
                    (is_odd, line, tile),
                )
                following = []
                for entries, count, (chosen, line, tile) in zip(lists, used, targets):

                    @pl.when(chosen)
                    def _(entries=entries, count=count, line=line, tile=tile):
                        entries[0, count] = line
                        entries[1, count] = where
                        entries[2, count] = tile

                    following.append(count + chosen.astype(jnp.int32))
                return tuple(following)

            used = lax.fori_loop(0, ints[rows, row], one, used)
    for entries, count in zip(lists, used):
        for extra in range(GROUP - 1):
            entries[0, count + extra] = 0
            entries[1, count + extra] = chip_rows * cap
            entries[2, count + extra] = 0
        entries[3, 0] = lax.div(count + GROUP - 1, GROUP)


def stage(pieces, halves):
    width = halves.shape[1] - 16
    at = 0
    for piece in pieces:
        tiles = piece.shape[0] // width
        for tile in range(tiles):
            high, low = split(piece[tile * width : (tile + 1) * width, :])
            halves[at, :width, :B] = high
            halves[at, :width, B:] = low
            row = piece[tiles * width + tile : tiles * width + tile + 1, :]
            high, low = split(jnp.concatenate([row, jnp.zeros((15, B), jnp.float32)], 0))
            halves[at, width:, :B] = high
            halves[at, width:, B:] = low
            at += 1


def multiply(entries, rhs, halves, total):
    def group(index, carry):
        for member in range(GROUP):
            at = index * GROUP + member
            row = entries[0, at]
            matrix = rhs[entries[1, at]]
            result = jnp.dot(
                halves[entries[2, at]],
                jnp.concatenate([matrix, matrix], 0),
                preferred_element_type=jnp.float32,
            )
            total[row] = total[row] + (result[:, :B] + result[:, B:])
        return carry

    lax.fori_loop(0, entries[3, 0], group, 0)


def near_kernel(even, odd, listed, rhs, even_total, odd_total, halves, total, entries, semaphore):
    copy = pltpu.make_async_copy(listed, entries, semaphore)
    copy.start()
    total[...] = jnp.zeros(total.shape, total.dtype)
    stage([even, odd], halves)
    copy.wait()
    multiply(entries, rhs, halves, total)
    even_total[...] = total[:REACH]
    odd_total[...] = total[REACH:]


def update(first, tile, state, before, total, width):
    here = slice(tile * width, (tile + 1) * width)
    check = slice(REACH * width + tile, REACH * width + tile + 1)
    pair = []
    for product, at in ((total[tile, :width, :], here), (total[tile, width : width + 1, :], check)):
        value = (product - CENTRE * state[at, :]) * (1.0 / HALF_WIDTH)
        if not first:
            value = 2.0 * value - before[at, :]
        pair.append(value)
    return pair


def far_products(near_total, halo, listed, rhs, halves, total, entries, semaphore):
    copy = pltpu.make_async_copy(listed, entries, semaphore)
    copy.start()
    total[...] = near_total[...]
    stage([halo], halves)
    copy.wait()
    multiply(entries, rhs, halves, total)
    return halves.shape[1] - 16


def far_kernel(first, state, before, near_total, halo, listed, rhs, out, halves, total, *lists):
    width = far_products(near_total, halo, listed, rhs, halves, total, *lists)
    for tile in range(REACH):
        main, row = update(first, tile, state, before, total, width)
        out[tile * width : (tile + 1) * width, :] = main
        out[REACH * width + tile : REACH * width + tile + 1, :] = row


def swap_here():
    return REACH * (1 - lax.axis_index("core"))


def part_from(steps):
    parts = lax.axis_size("part")
    return lax.rem(lax.axis_index("part") + steps * (1 - 2 * lax.axis_index("core")) + parts, parts)


def last_kernel(state, before, near_total, halo, listed, rhs, odd, *refs):
    halves, total, entries, semaphore, keep = refs[-5:]
    outs, checks = refs[:-6], refs[-6]
    parts = len(outs)
    width = far_products(near_total, halo, listed, rhs, halves, total, entries, semaphore)
    each = width // parts
    swap = swap_here()
    even_at, odd_at = swap, REACH - swap
    for tile in range(REACH):
        main, row = update(False, tile, state, before, total, width)
        keep[tile * width : (tile + 1) * width, :] = main
        checks[pl.ds(even_at + tile, 1), :] = row
        spot = REACH * width + tile
        checks[pl.ds(odd_at + tile, 1), :] = odd[spot : spot + 1, :]
    for steps, out in enumerate(outs):
        at = pl.multiple_of(part_from(steps) * each, each)
        for tile in range(REACH):
            out[even_at + tile] = keep[pl.ds(tile * width + at, each), :]
            out[odd_at + tile] = odd[pl.ds(tile * width + at, each), :]


def gather_kernel(order, weights, *refs):
    del order
    parts = weights.shape[0] // refs[0].shape[1]
    pieces, halves = refs[:parts], refs[parts:]
    each = pieces[0].shape[1]
    width = parts * each
    for half, start in zip(halves, (swap_here(), REACH - swap_here())):
        for tile in range(REACH):
            row = jnp.zeros((1, B), jnp.float32)
            for steps, piece in enumerate(pieces):
                at = pl.multiple_of(part_from(-steps) * each, each)
                value = piece[start + tile]
                row = row + jnp.sum(value * weights[pl.ds(at, each), :], axis=0, keepdims=True)
                half[pl.ds(tile * width + at, each), :] = value
            spot = REACH * width + tile
            half[spot : spot + 1, :] = row


def arrange_kernel(vectors, *refs):
    pieces, semaphores = refs[:-1], refs[-1]
    parts, tiles = len(pieces), pieces[0].shape[0]
    copies = []
    for steps in (*range(1, parts), 0):
        at = part_from(steps) * (tiles * B)
        for tile in range(tiles):
            lanes = pl.ds(pl.multiple_of(at + tile * B, B), B)
            semaphore = semaphores.at[steps * tiles + tile]
            copies.append(
                pltpu.make_async_copy(vectors.at[:, lanes], pieces[steps].at[tile], semaphore)
            )
    for copy in copies:
        copy.start()
    for copy in copies:
        copy.wait()


def place_kernel(checks, other_checks, *refs):
    pieces, (out, out_check) = refs[:-2], refs[-2:]
    parts, tiles = len(pieces), pieces[0].shape[0]
    for steps, piece in enumerate(pieces):
        at = part_from(-steps) * (tiles * B)
        for tile in range(tiles):
            out[:, pl.ds(pl.multiple_of(at + tile * B, B), B)] = piece[tile]
    rows = out_check.shape[0]
    for row in range(rows):
        line = pl.ds(lax.axis_index("core") * rows + row, 1)
        out_check[row : row + 1, :] = checks[line, :] + other_checks[line, :]


def call(kernel, shapes, inputs, scratch=(), flops=1, moved=1):
    return pl.pallas_call(
        kernel,
        out_shape=tuple(jax.ShapeDtypeStruct(shape, dtype) for shape, dtype, _ in shapes),
        in_specs=[spec for _, spec in inputs],
        out_specs=tuple(spec for _, _, spec in shapes),
        scratch_shapes=list(scratch),
        compiler_params=pltpu.CompilerParams(vmem_limit_bytes=16 << 20),
        cost_estimate=pl.CostEstimate(flops=flops, bytes_accessed=moved, transcendentals=0),
    )(*[value for value, _ in inputs])


def shift(value, axes, count, steps):
    return lax.ppermute(value, axes, [(at, (at + steps) % count) for at in range(count)])


def per_device(start_vectors, ham_blocks, block_cols, block_counts, check_weights):
    f32 = jnp.float32
    rows, cap = ham_blocks.shape[0], ham_blocks.shape[1]
    parts = lax.axis_size("part")
    chips = lax.axis_size(("row", "part"))
    core = lax.axis_index("core")
    chip = lax.axis_index(("row", "part"))
    tiles = CORES * rows
    total = chips * tiles
    each = start_vectors.shape[1]
    width = parts * each

    swap = REACH * (1 - core)
    place = jnp.stack([core, chip * tiles, lax.axis_index("part"), swap]).astype(jnp.int32)

    def pairs(count, steps):
        return [
            (at * CORES + side, (at + steps * (1 - 2 * side)) % count * CORES + side)
            for at in range(count)
            for side in range(CORES)
        ]

    def exchange(pieces):
        moved = [
            lax.ppermute(pieces[steps], ("part", "core"), pairs(parts, steps))
            for steps in range(1, parts)
        ]
        return [pieces[0]] + moved

    def round_chips(value, steps):
        return lax.ppermute(value, ("row", "part", "core"), pairs(chips, steps))

    piece = ((tiles, each, B), f32, VMEM)
    copies = pltpu.SemaphoreType.DMA((parts * tiles,))
    sent = call(arrange_kernel, (piece,) * parts, [(pltpu.with_memory_space_constraint(start_vectors.T, pltpu.HBM), HBM)], [copies])
    arrived = exchange(sent)
    blocks, columns, counts, _ = lax.optimization_barrier(
        (ham_blocks, block_cols, block_counts, sent[0])
    )
    ints = jnp.concatenate([columns, jnp.pad(counts, (0, cap - rows))[None, :]], 0)
    other_ints = shift(ints, "core", CORES, 1)
    other_blocks = shift(blocks, "core", CORES, 1)
    list_shape = ((4, tiles * cap + GROUP), jnp.int32, SMEM)
    rhs, near_list, even_list, odd_list = call(
        functools.partial(prepare_kernel, total),
        (((tiles * cap + 1, B, 2 * B), jnp.bfloat16, VMEM), list_shape, list_shape, list_shape),
        [(place, SMEM), (ints, SMEM), (other_ints, SMEM), (pltpu.with_memory_space_constraint(ham_blocks, pltpu.HBM), HBM), (other_blocks, VMEM)],
        [pltpu.VMEM(ham_blocks.shape, f32), pltpu.SemaphoreType.DMA((rows,))],
    )
    mine = lax.dynamic_index_in_dim(check_weights.reshape(parts, CORES, each), core, 1, False)
    weights = jnp.broadcast_to(mine.reshape(width, 1), (width, B))
    full = ((REACH * width + CHECK, B), f32, VMEM)
    even, odd = call(
        gather_kernel,
        (full, full),
        [(near_list, ANY), (weights, VMEM)] + [(value, VMEM) for value in arrived],
    )
    even_before, odd_before = even, odd
    list_scratch = [pltpu.SMEM(list_shape[0], jnp.int32), pltpu.SemaphoreType.DMA(())]
    part_total = ((REACH, width + 16, B), f32, VMEM)
    scratch = [
        pltpu.VMEM((REACH, width + 16, 2 * B), jnp.bfloat16),
        pltpu.VMEM((REACH, width + 16, B), f32),
    ] + list_scratch
    for step in range(ITERS):
        first, last = step == 0, step == ITERS - 1
        odd_halo = round_chips(even, 1)
        even_halo = round_chips(odd, -1)
        even_total, odd_total = call(
            near_kernel,
            (part_total, part_total),
            [(even, VMEM), (odd, VMEM), (near_list, ANY), (rhs, VMEM)],
            [
                pltpu.VMEM((tiles, width + 16, 2 * B), jnp.bfloat16),
                pltpu.VMEM((tiles, width + 16, B), f32),
            ]
            + list_scratch,
        )

        def inputs(state, before, near_total, halo, entries):
            values = (state, before, near_total, halo)
            return [(value, VMEM) for value in values] + [(entries, ANY), (rhs, VMEM)]

        kernel = functools.partial(far_kernel, first)
        (odd_next,) = call(
            kernel, (full,), inputs(odd, odd_before, odd_total, odd_halo, odd_list), scratch
        )
        even_inputs = inputs(even, even_before, even_total, even_halo, even_list)
        if last:
            *outs, checks = call(
                last_kernel,
                (piece,) * parts + (((tiles, B), f32, VMEM),),
                even_inputs + [(odd_next, VMEM)],
                scratch + [pltpu.VMEM((REACH * width, B), f32)],
            )
            break
        (even_next,) = call(kernel, (full,), even_inputs, scratch)
        even_before, odd_before = even, odd
        even, odd = even_next, odd_next
    returned = exchange(outs)
    filtered, check_sums = call(
        place_kernel,
        (((each, parts * tiles * B), f32, VMEM), ((rows, B), f32, VMEM)),
        [(checks, VMEM), (shift(checks, "core", CORES, 1), VMEM)]
        + [(value, VMEM) for value in returned],
    )
    return filtered.T, check_sums.reshape(rows * B)


def solution(mesh):
    names = ("row", "part", "core")
    rows, cols = mesh.devices.shape
    finer = Mesh(mesh.devices.reshape(rows, cols // CORES, CORES), names)
    placed = (
        P("row", ("part", "core")),
        P(names, None, None, None),
        P(names, None),
        P(names),
        P(),
    )
    return jax.shard_map(
        per_device,
        mesh=finer,
        in_specs=placed,
        out_specs=(P("row", ("part", "core")), P(names)),
        check_vma=False,
    )
```

```python
import functools

import jax
import jax.numpy as jnp
from jax import lax
from jax.experimental import pallas as pl
from jax.experimental.pallas import tpu as pltpu
from jax.sharding import Mesh
from jax.sharding import PartitionSpec as P

REACH = 4
ITERS = 3
CENTRE = 0.25
HALF_WIDTH = 1.5
B = 128
CORES = 2
GROUP = 4
CHECK = 8

VMEM = pl.BlockSpec(memory_space=pltpu.VMEM)
SMEM = pl.BlockSpec(memory_space=pltpu.SMEM)
ANY = pl.BlockSpec(memory_space=pl.ANY)
HBM = pl.BlockSpec(memory_space=pltpu.HBM)


def split(value):
    high = value.astype(jnp.bfloat16)
    low = (value - high.astype(jnp.float32)).astype(jnp.bfloat16)
    return high, low


def prepare_kernel(
    total, place, ints_own, ints_other, source, other, rhs, near_list, even_list, odd_list, own, semaphores
):
    rows, cap = own.shape[0], own.shape[1]
    copies = [
        pltpu.make_async_copy(source.at[row], own.at[row], semaphores.at[row]) for row in range(rows)
    ]
    for copy in copies:
        copy.start()
    core, base, swap = place[0], place[1], place[3]
    chip_rows = CORES * rows
    rhs[chip_rows * cap] = jnp.zeros(rhs.shape[1:], rhs.dtype)
    lists = (near_list, even_list, odd_list)
    used = (jnp.int32(0),) * 3
    for ints, blocks, side in ((ints_other, other, 1 - core), (ints_own, own, core)):
        for row in range(rows):
            if blocks is own:
                copies[row].wait()
            chip_row = side * rows + row

            def one(slot, used, ints=ints, blocks=blocks, row=row, chip_row=chip_row):
                high, low = split(blocks[row, slot].T)
                where = chip_row * cap + slot
                rhs[where, :, :B] = high
                rhs[where, :, B:] = low
                column = lax.rem(ints[row, slot] - base + total + total, total)
                is_left = column >= total - REACH
                is_near = column < chip_rows
                tile = jnp.where(is_left, column - (total - REACH), column - chip_rows)
                is_even = jnp.logical_and(jnp.logical_not(is_near), is_left == (swap == 0))
                is_odd = jnp.logical_and(jnp.logical_not(is_near), is_left != (swap == 0))
                line = lax.rem(chip_row, REACH)
                targets = (
                    (is_near, lax.rem(chip_row + swap, 2 * REACH), lax.rem(column + swap, 2 * REACH)),
                    (is_even, line, tile),
                    (is_odd, line, tile),
                )
                following = []
                for entries, count, (chosen, line, tile) in zip(lists, used, targets):

                    @pl.when(chosen)
                    def _(entries=entries, count=count, line=line, tile=tile):
                        entries[0, count] = line
                        entries[1, count] = where
                        entries[2, count] = tile

                    following.append(count + chosen.astype(jnp.int32))
                return tuple(following)

            used = lax.fori_loop(0, ints[rows, row], one, used)
    for entries, count in zip(lists, used):
        for extra in range(GROUP - 1):
            entries[0, count + extra] = 0
            entries[1, count + extra] = chip_rows * cap
            entries[2, count + extra] = 0
        entries[3, 0] = lax.div(count + GROUP - 1, GROUP)


def stage(pieces, halves):
    width = halves.shape[1] - 16
    at = 0
    for piece in pieces:
        tiles = piece.shape[0] // width
        for tile in range(tiles):
            high, low = split(piece[tile * width : (tile + 1) * width, :])
            halves[at, :width, :B] = high
            halves[at, :width, B:] = low
            row = piece[tiles * width + tile : tiles * width + tile + 1, :]
            high, low = split(jnp.concatenate([row, jnp.zeros((15, B), jnp.float32)], 0))
            halves[at, width:, :B] = high
            halves[at, width:, B:] = low
            at += 1


def multiply(entries, rhs, halves, total):
    def group(index, carry):
        for member in range(GROUP):
            at = index * GROUP + member
            row = entries[0, at]
            matrix = rhs[entries[1, at]]
            result = jnp.dot(
                halves[entries[2, at]],
                jnp.concatenate([matrix, matrix], 0),
                preferred_element_type=jnp.float32,
            )
            total[row] = total[row] + (result[:, :B] + result[:, B:])
        return carry

    lax.fori_loop(0, entries[3, 0], group, 0)


def near_kernel(even, odd, listed, rhs, even_total, odd_total, halves, total, entries, semaphore):
    copy = pltpu.make_async_copy(listed, entries, semaphore)
    copy.start()
    total[...] = jnp.zeros(total.shape, total.dtype)
    stage([even, odd], halves)
    copy.wait()
    multiply(entries, rhs, halves, total)
    even_total[...] = total[:REACH]
    odd_total[...] = total[REACH:]


def update(first, tile, state, before, total, width):
    here = slice(tile * width, (tile + 1) * width)
    check = slice(REACH * width + tile, REACH * width + tile + 1)
    pair = []
    for product, at in ((total[tile, :width, :], here), (total[tile, width : width + 1, :], check)):
        value = (product - CENTRE * state[at, :]) * (1.0 / HALF_WIDTH)
        if not first:
            value = 2.0 * value - before[at, :]
        pair.append(value)
    return pair


def far_products(near_total, halo, listed, rhs, halves, total, entries, semaphore):
    copy = pltpu.make_async_copy(listed, entries, semaphore)
    copy.start()
    total[...] = near_total[...]
    stage([halo], halves)
    copy.wait()
    multiply(entries, rhs, halves, total)
    return halves.shape[1] - 16


def far_kernel(first, state, before, near_total, halo, listed, rhs, out, halves, total, *lists):
    width = far_products(near_total, halo, listed, rhs, halves, total, *lists)
    for tile in range(REACH):
        main, row = update(first, tile, state, before, total, width)
        out[tile * width : (tile + 1) * width, :] = main
        out[REACH * width + tile : REACH * width + tile + 1, :] = row


def swap_here():
    return REACH * (1 - lax.axis_index("core"))


def part_from(steps):
    parts = lax.axis_size("part")
    return lax.rem(lax.axis_index("part") + steps * (1 - 2 * lax.axis_index("core")) + parts, parts)


def last_kernel(state, before, near_total, halo, listed, rhs, odd, *refs):
    halves, total, entries, semaphore, keep = refs[-5:]
    outs, checks = refs[:-6], refs[-6]
    parts = len(outs)
    width = far_products(near_total, halo, listed, rhs, halves, total, entries, semaphore)
    each = width // parts
    swap = swap_here()
    even_at, odd_at = swap, REACH - swap
    for tile in range(REACH):
        main, row = update(False, tile, state, before, total, width)
        keep[tile * width : (tile + 1) * width, :] = main
        checks[pl.ds(even_at + tile, 1), :] = row
        spot = REACH * width + tile
        checks[pl.ds(odd_at + tile, 1), :] = odd[spot : spot + 1, :]
    for steps, out in enumerate(outs):
        at = pl.multiple_of(part_from(steps) * each, each)
        for tile in range(REACH):
            out[even_at + tile] = keep[pl.ds(tile * width + at, each), :]
            out[odd_at + tile] = odd[pl.ds(tile * width + at, each), :]


def gather_kernel(order, weights, *refs):
    del order
    parts, (column, line, semaphore) = lax.axis_size("part"), refs[-3:]
    pieces, halves = refs[:parts], refs[parts:-3]
    copy = pltpu.make_async_copy(weights, line, semaphore)
    copy.start()
    each = pieces[0].shape[1]
    width = parts * each
    starts = (swap_here(), REACH - swap_here())
    for half, start in zip(halves, starts):
        for steps, piece in enumerate(pieces):
            at = pl.multiple_of(part_from(-steps) * each, each)
            for tile in range(REACH):
                half[pl.ds(tile * width + at, each), :] = piece[start + tile]
    copy.wait()
    shape = (B, line.shape[1])
    for first in range(0, line.shape[1], B):
        at = first + lax.broadcasted_iota(jnp.int32, shape, 0)
        chosen = at == lax.broadcasted_iota(jnp.int32, shape, 1)
        value = jnp.sum(jnp.where(chosen, line[...], 0.0), axis=1, keepdims=True)
        column[first : first + B, :] = jnp.broadcast_to(value, (B, B))
    for half, start in zip(halves, starts):
        rows = [jnp.zeros((1, B), jnp.float32)] * REACH
        for steps, piece in enumerate(pieces):
            group = (part_from(-steps) * CORES + lax.axis_index("core")) * each
            factors = column[pl.ds(pl.multiple_of(group, each), each), :]
            for tile in range(REACH):
                terms = piece[start + tile] * factors
                rows[tile] = rows[tile] + jnp.sum(terms, axis=0, keepdims=True)
        for tile in range(REACH):
            half[REACH * width + tile : REACH * width + tile + 1, :] = rows[tile]


def arrange_kernel(vectors, *refs):
    pieces, semaphores = refs[:-1], refs[-1]
    parts, tiles = len(pieces), pieces[0].shape[0]
    copies = []
    for steps in (*range(1, parts), 0):
        at = part_from(steps) * (tiles * B)
        for tile in range(tiles):
            lanes = pl.ds(pl.multiple_of(at + tile * B, B), B)
            semaphore = semaphores.at[steps * tiles + tile]
            copies.append(
                pltpu.make_async_copy(vectors.at[:, lanes], pieces[steps].at[tile], semaphore)
            )
    for copy in copies:
        copy.start()
    for copy in copies:
        copy.wait()


def place_kernel(checks, other_checks, *refs):
    pieces, (out, out_check) = refs[:-2], refs[-2:]
    parts, tiles = len(pieces), pieces[0].shape[0]
    for steps, piece in enumerate(pieces):
        at = part_from(-steps) * (tiles * B)
        for tile in range(tiles):
            out[:, pl.ds(pl.multiple_of(at + tile * B, B), B)] = piece[tile]
    rows = out_check.shape[0]
    for row in range(rows):
        line = pl.ds(lax.axis_index("core") * rows + row, 1)
        out_check[row : row + 1, :] = checks[line, :] + other_checks[line, :]


def call(kernel, shapes, inputs, scratch=(), flops=1, moved=1):
    return pl.pallas_call(
        kernel,
        out_shape=tuple(jax.ShapeDtypeStruct(shape, dtype) for shape, dtype, _ in shapes),
        in_specs=[spec for _, spec in inputs],
        out_specs=tuple(spec for _, _, spec in shapes),
        scratch_shapes=list(scratch),
        compiler_params=pltpu.CompilerParams(vmem_limit_bytes=16 << 20),
        cost_estimate=pl.CostEstimate(flops=flops, bytes_accessed=moved, transcendentals=0),
    )(*[value for value, _ in inputs])


def shift(value, axes, count, steps):
    return lax.ppermute(value, axes, [(at, (at + steps) % count) for at in range(count)])


def per_device(start_vectors, ham_blocks, block_cols, block_counts, check_weights):
    f32 = jnp.float32
    rows, cap = ham_blocks.shape[0], ham_blocks.shape[1]
    parts = lax.axis_size("part")
    chips = lax.axis_size(("row", "part"))
    core = lax.axis_index("core")
    chip = lax.axis_index(("row", "part"))
    tiles = CORES * rows
    total = chips * tiles
    each = start_vectors.shape[1]
    width = parts * each

    swap = REACH * (1 - core)
    place = jnp.stack([core, chip * tiles, lax.axis_index("part"), swap]).astype(jnp.int32)

    def pairs(count, steps):
        return [
            (at * CORES + side, (at + steps * (1 - 2 * side)) % count * CORES + side)
            for at in range(count)
            for side in range(CORES)
        ]

    def exchange(pieces):
        moved = [
            lax.ppermute(pieces[steps], ("part", "core"), pairs(parts, steps))
            for steps in range(1, parts)
        ]
        return [pieces[0]] + moved

    def round_chips(value, steps):
        return lax.ppermute(value, ("row", "part", "core"), pairs(chips, steps))

    piece = ((tiles, each, B), f32, VMEM)
    copies = pltpu.SemaphoreType.DMA((parts * tiles,))
    sent = call(arrange_kernel, (piece,) * parts, [(pltpu.with_memory_space_constraint(start_vectors.T, pltpu.HBM), HBM)], [copies])
    arrived = exchange(sent)
    blocks, columns, counts, _ = lax.optimization_barrier(
        (ham_blocks, block_cols, block_counts, sent[0])
    )
    ints = jnp.concatenate([columns, jnp.pad(counts, (0, cap - rows))[None, :]], 0)
    other_ints = shift(ints, "core", CORES, 1)
    other_blocks = shift(blocks, "core", CORES, 1)
    list_shape = ((4, tiles * cap + GROUP), jnp.int32, SMEM)
    rhs, near_list, even_list, odd_list = call(
        functools.partial(prepare_kernel, total),
        (((tiles * cap + 1, B, 2 * B), jnp.bfloat16, VMEM), list_shape, list_shape, list_shape),
        [(place, SMEM), (ints, SMEM), (other_ints, SMEM), (pltpu.with_memory_space_constraint(ham_blocks, pltpu.HBM), HBM), (other_blocks, VMEM)],
        [pltpu.VMEM(ham_blocks.shape, f32), pltpu.SemaphoreType.DMA((rows,))],
    )
    full = ((REACH * width + CHECK, B), f32, VMEM)
    even, odd = call(
        gather_kernel,
        (full, full),
        [(other_ints, ANY), (pltpu.with_memory_space_constraint(check_weights[None, :], pltpu.HBM), HBM)]
        + [(value, VMEM) for value in arrived],
        [
            pltpu.VMEM((check_weights.shape[0], B), f32),
            pltpu.VMEM((1, check_weights.shape[0]), f32),
            pltpu.SemaphoreType.DMA(()),
        ],
    )
    even_before, odd_before = even, odd
    list_scratch = [pltpu.SMEM(list_shape[0], jnp.int32), pltpu.SemaphoreType.DMA(())]
    part_total = ((REACH, width + 16, B), f32, VMEM)
    scratch = [
        pltpu.VMEM((REACH, width + 16, 2 * B), jnp.bfloat16),
        pltpu.VMEM((REACH, width + 16, B), f32),
    ] + list_scratch
    for step in range(ITERS):
        first, last = step == 0, step == ITERS - 1
        odd_halo = round_chips(even, 1)
        even_halo = round_chips(odd, -1)
        even_total, odd_total = call(
            near_kernel,
            (part_total, part_total),
            [(even, VMEM), (odd, VMEM), (near_list, ANY), (rhs, VMEM)],
            [
                pltpu.VMEM((tiles, width + 16, 2 * B), jnp.bfloat16),
                pltpu.VMEM((tiles, width + 16, B), f32),
            ]
            + list_scratch,
        )

        def inputs(state, before, near_total, halo, entries):
            values = (state, before, near_total, halo)
            return [(value, VMEM) for value in values] + [(entries, ANY), (rhs, VMEM)]

        kernel = functools.partial(far_kernel, first)
        (odd_next,) = call(
            kernel, (full,), inputs(odd, odd_before, odd_total, odd_halo, odd_list), scratch
        )
        even_inputs = inputs(even, even_before, even_total, even_halo, even_list)
        if last:
            *outs, checks = call(
                last_kernel,
                (piece,) * parts + (((tiles, B), f32, VMEM),),
                even_inputs + [(odd_next, VMEM)],
                scratch + [pltpu.VMEM((REACH * width, B), f32)],
            )
            break
        (even_next,) = call(kernel, (full,), even_inputs, scratch)
        even_before, odd_before = even, odd
        even, odd = even_next, odd_next
    returned = exchange(outs)
    filtered, check_sums = call(
        place_kernel,
        (((each, parts * tiles * B), f32, VMEM), ((rows, B), f32, VMEM)),
        [(checks, VMEM), (shift(checks, "core", CORES, 1), VMEM)]
        + [(value, VMEM) for value in returned],
    )
    return filtered.T, check_sums.reshape(rows * B)


def solution(mesh):
    names = ("row", "part", "core")
    rows, cols = mesh.devices.shape
    finer = Mesh(mesh.devices.reshape(rows, cols // CORES, CORES), names)
    placed = (
        P("row", ("part", "core")),
        P(names, None, None, None),
        P(names, None),
        P(names),
        P(),
    )
    return jax.shard_map(
        per_device,
        mesh=finer,
        in_specs=placed,
        out_specs=(P("row", ("part", "core")), P(names)),
        check_vma=False,
    )
```
